32 devices in a mesh: frame: 8 (over y, x, core), head: 4 (over z).
Axes of the slice: x: 2, y: 2, z: 4, core: 2. Of those that a mesh axis runs over, the one named last changes fastest.
Arguments:
- queries: bfloat16 [4, 2048, 4096], P(None, 'frame', 'head'), may hold values from -6 to 6
- keys: bfloat16 [4, 2048, 4096], P(None, 'frame', 'head'), may hold values from -6 to 6
- values: bfloat16 [4, 2048, 4096], P(None, 'frame', 'head'), may hold values from -6 to 6
- step_sizes: bfloat16 [4, 2048, 16], P(None, 'frame', 'head'), may hold values from 9e-05 to 1.25, as said below
- starts: int32 [4], replicated, may hold values from 0 to 7, as said below
- resets: int32 [4, 8], replicated, may hold values 0 or 1
- init_in: bfloat16 [16, 256, 1024], P('head'), may hold values from -0.375 to 0.375
- init_out: bfloat16 [16, 512, 256], P('head'), may hold values from -0.25 to 0.25
- gain: float32 [4096], P('head'), may hold values from 0.25 to 1.75
- out_proj: bfloat16 [4096, 5120], P('head'), may hold values from -0.125 to 0.125
Outputs:
- mixed_out: bfloat16 [4, 2048, 5120], P(None, 'frame', 'head')
The draws below stay inside these ranges and needn't reach their ends.
Inputs may be any that keep to these rules, and one draw needn't show every extreme that they name: `starts`: 4 distinct blocks. `step_sizes`: positive.
All inputs are finite; a program needn't handle non-finite values.
Results may differ from the reference program's by a relative error of at most 0.035.
Values may be sent and summed in bfloat16 or wider, within the bound.
No kernel may reach another device: no remote copies, remote signals or barrier semaphores. Data moves between devices by JAX's collectives and lax.ppermute only.
A program may use at most 128 MiB of HBM per device.

```python
import math
import jax
import jax.numpy as jnp
from jax import lax

HS = 256
HID = 512
HEADS = 16
DW = 5120
VIDEO_COUNT = 4
SEG_ROWS = 256
SEGS = 8
VIDEO_TOKENS = 2048
N_HEAD = 4


def draw_step_sizes(key, part):
    random_key_base, random_key_noise, random_key_spikes = jax.random.split(key, 3)
    learning_rate_base = jnp.exp(jax.random.uniform(random_key_base, (VIDEO_COUNT, 1, HEADS), jnp.float32, math.log(0.0002), math.log(0.02)))
    random_noise = jnp.exp(jax.random.uniform(random_key_noise, (VIDEO_COUNT, VIDEO_TOKENS, HEADS), jnp.float32, math.log(0.5), math.log(2.0)))
    sudden_spikes = jnp.where(jax.random.uniform(random_key_spikes, (VIDEO_COUNT, VIDEO_TOKENS, 1), jnp.float32) < 3.0 / VIDEO_TOKENS, 30.0, 1.0)
    return (learning_rate_base * random_noise * sudden_spikes).astype(jnp.bfloat16)


def draw_starts(key, part):
    order = jax.random.permutation(jax.random.fold_in(key, 17), SEGS)
    return order[:VIDEO_COUNT].astype(jnp.int32)


def place_ends(result, key, least, high):
    spot = [jax.random.randint(jax.random.fold_in(key, axis), (), 0, length) for axis, length in enumerate(result.shape)]
    widest = result.shape.index(max(result.shape))
    next_to = spot[:widest] + [(spot[widest] + 1) % result.shape[widest]] + spot[widest + 1:]
    return result.at[tuple(spot)].set(least).at[tuple(next_to)].set(high)


def raised(values, key, source, target, parts, factor):
    owner, partner = [(jnp.arange(values.shape[axis_at]) // (values.shape[axis_at] // parts)).reshape([-1 if axis == axis_at else 1 for axis in range(values.ndim)]) for axis_at in (source, target)]
    chosen = jax.random.permutation(key, parts)[partner]
    strong = (owner == chosen) | (owner == (partner + parts // 2) % parts)
    return jnp.where(strong, factor * values, values)


def block_scale(own_key, extent, pieces, smallest, top_value):
    def one(dim, blocks):
        draws = jax.random.uniform(jax.random.fold_in(jax.random.fold_in(own_key, 6), dim), (blocks,), jnp.float32, smallest / len(pieces), top_value / len(pieces))
        return jnp.repeat(jnp.exp(draws), extent[dim] // blocks).reshape((-1,) + (1,) * (len(extent) - dim - 1))

    level = one(*pieces[0])
    for cut in pieces[1:]:
        level = level * one(*cut)
    return level


def gaussian(key, extent, deviation, reach, pieces=(), kind=jnp.bfloat16):
    drawn = jax.random.normal(key, extent, jnp.float32) * deviation
    if len(pieces) > 0:
        drawn = block_scale(key, extent, pieces, -0.22, 0.18) * drawn
    return jnp.clip(drawn, min=-reach, max=reach).astype(kind)


def noise_with(key, extent, scale, limit, shards, heavy, kind=jnp.bfloat16):
    entries = scale * jax.random.normal(key, extent, jnp.float32)
    if shards:
        entries = entries * block_scale(key, extent, shards, -0.22, 0.18)
    return jnp.clip(raised(entries, jax.random.fold_in(key, 3), *heavy), -limit, limit).astype(kind)


def setup_inputs(seed: int = 0) -> dict:
    arg_keys = jax.random.split(jax.random.key(seed), 11)
    queries = gaussian(arg_keys[0], (VIDEO_COUNT, VIDEO_TOKENS, HEADS * HS), 1.0, 6.0, ((1, 8), (2, 4)))
    keys = gaussian(arg_keys[1], (VIDEO_COUNT, VIDEO_TOKENS, HEADS * HS), 1.0, 6.0, ((1, 8), (2, 4)))
    values = gaussian(arg_keys[2], (VIDEO_COUNT, VIDEO_TOKENS, HEADS * HS), 1.0, 6.0, ((1, 8), (2, 4)))
    step_sizes = draw_step_sizes(jax.random.fold_in(arg_keys[10], 71), 0)
    starts = draw_starts(jax.random.fold_in(arg_keys[10], 71), 0)
    resets = place_ends((jax.random.randint(arg_keys[5], (VIDEO_COUNT, SEGS), 0, 4) < 1).astype(jnp.int32), jax.random.fold_in(arg_keys[5], 1), 0, 1)
    init_in = gaussian(arg_keys[6], (HEADS, HS, 2 * HID), HS ** -0.5, 0.375, ((0, 4),))
    init_out = gaussian(arg_keys[7], (HEADS, HID, HS), HID ** -0.5, 0.25, ((0, 4),))
    gain = jnp.clip(1.0 + 0.15 * jax.random.normal(arg_keys[8], (HEADS * HS,), jnp.float32), 0.25, 1.75)
    out_proj = noise_with(arg_keys[9], (HEADS * HS, DW), (HEADS * HS) ** -0.5, 0.125, ((0, 4),), (0, 1, 4, 2.0))
    return dict(queries=queries, keys=keys, values=values, step_sizes=step_sizes, starts=starts, resets=resets, init_in=init_in, init_out=init_out, gain=gain, out_proj=out_proj)


def renorm(raw_weights, target):
    column_scale = target[:, None, :] * lax.rsqrt(lax.optimization_barrier(jnp.sum(raw_weights * raw_weights, axis=1, keepdims=True)) + 1e-06)
    return (raw_weights * column_scale).astype(jnp.bfloat16)

def advance(weights_in, weights_out, queries_seg, keys_seg, values_seg, rates_seg, norm_in, norm_out, gain):
    rows_here = queries_seg.shape[0]
    heads_here = weights_in.shape[0]
    head_width = weights_in.shape[1]
    hidden_width = weights_out.shape[1]
    key_heads = keys_seg.reshape(rows_here, heads_here, head_width).astype(jnp.float32)
    pre_keys = jnp.einsum('thd,hde->hte', key_heads, weights_in.astype(jnp.float32))
    first_half = pre_keys[..., :hidden_width]
    second_half = pre_keys[..., hidden_width:]
    sigmoid_first = jax.nn.sigmoid(first_half)
    activated = first_half * sigmoid_first
    hidden = (activated * second_half).astype(jnp.bfloat16)
    value_heads = values_seg.reshape(rows_here, heads_here, head_width).astype(jnp.float32)
    scaled = (value_heads * rates_seg.astype(jnp.float32)[:, :, None]).astype(jnp.bfloat16)
    grad_hidden = jnp.einsum('the,hfe->htf', scaled.astype(jnp.float32), weights_out.astype(jnp.float32))
    grad_first = grad_hidden * second_half * sigmoid_first * (1.0 + first_half * (1.0 - sigmoid_first))
    grad_second = grad_hidden * activated
    grad_pre = jnp.concatenate([grad_first, grad_second], axis=-1).astype(jnp.bfloat16)
    raw_in = weights_in.astype(jnp.float32) + jnp.einsum('thd,hte->hde', key_heads, grad_pre.astype(jnp.float32))
    raw_out = weights_out.astype(jnp.float32) + jnp.einsum('htf,the->hfe', hidden.astype(jnp.float32), scaled.astype(jnp.float32))
    new_in = renorm(raw_in, norm_in)
    new_out = renorm(raw_out, norm_out)
    query_heads = queries_seg.reshape(rows_here, heads_here, head_width).astype(jnp.float32)
    pre_queries = jnp.einsum('thd,hde->hte', query_heads, new_in.astype(jnp.float32))
    hidden_queries = (jax.nn.silu(pre_queries[..., :hidden_width]) * pre_queries[..., hidden_width:]).astype(jnp.bfloat16)
    fast_out = jnp.einsum('htf,hfe->the', hidden_queries.astype(jnp.float32), new_out.astype(jnp.float32))
    normed = fast_out * lax.rsqrt(lax.optimization_barrier(jnp.mean(fast_out * fast_out, axis=-1, keepdims=True)) + 1e-05)
    normed = normed * gain.reshape(heads_here, head_width)
    return (new_in, new_out, normed.reshape(rows_here, heads_here * head_width).astype(jnp.bfloat16))

def reference(queries, keys, values, step_sizes, starts, resets, init_in, init_out, gain, out_proj):
    norm_in = jnp.sqrt(lax.optimization_barrier(jnp.sum(jnp.square(init_in.astype(jnp.float32)), axis=1)))
    norm_out = jnp.sqrt(lax.optimization_barrier(jnp.sum(jnp.square(init_out.astype(jnp.float32)), axis=1)))

    def one_video(video_queries, video_keys, video_values, video_rates, first_block, reset_flags):

        def segment(loop_state, seg_index):
            state_in, state_out = loop_state
            block_now = (first_block + seg_index) % SEGS
            first_row = (block_now * SEG_ROWS).astype(jnp.int32)
            queries_seg = lax.dynamic_slice_in_dim(video_queries, first_row, SEG_ROWS, 0)
            keys_seg = lax.dynamic_slice_in_dim(video_keys, first_row, SEG_ROWS, 0)
            values_seg = lax.dynamic_slice_in_dim(video_values, first_row, SEG_ROWS, 0)
            rates_seg = lax.dynamic_slice_in_dim(video_rates, first_row, SEG_ROWS, 0)
            restart = jnp.logical_or(seg_index == 0, reset_flags[seg_index] == 1)
            weights_in = jnp.where(restart, init_in, state_in)
            weights_out = jnp.where(restart, init_out, state_out)
            new_in, new_out, normed = advance(weights_in, weights_out, queries_seg, keys_seg, values_seg, rates_seg, norm_in, norm_out, gain)
            return ((new_in, new_out), normed)
        _, outputs = lax.scan(segment, (init_in, init_out), jnp.arange(SEGS, dtype=jnp.int32))
        return jnp.roll(outputs, first_block, axis=0).reshape(VIDEO_TOKENS, HEADS * HS)
    normed_all = jax.vmap(one_video)(queries, keys, values, step_sizes, starts, resets)
    flat_rows = normed_all.reshape(VIDEO_COUNT * VIDEO_TOKENS, HEADS * HS)
    group_width = HEADS * HS // N_HEAD

    def add_group(running, group_index):
        slice_rows = lax.dynamic_slice_in_dim(flat_rows, (group_index * group_width).astype(jnp.int32), group_width, 1)
        slice_weights = lax.dynamic_slice_in_dim(out_proj, (group_index * group_width).astype(jnp.int32), group_width, 0)
        partial_value = jnp.dot(slice_rows, slice_weights, preferred_element_type=jnp.float32).astype(jnp.bfloat16)
        partial_value = lax.optimization_barrier(partial_value)
        return (running + partial_value.astype(jnp.float32), None)
    running, _ = lax.scan(add_group, jnp.zeros((VIDEO_COUNT * VIDEO_TOKENS, DW), jnp.float32), jnp.arange(N_HEAD, dtype=jnp.int32))
    return running.astype(jnp.bfloat16).reshape(VIDEO_COUNT, VIDEO_TOKENS, DW)
```

```python
import functools

import jax
import jax.numpy as jnp
from jax import lax
from jax.experimental import pallas as pl
from jax.experimental.pallas import tpu as pltpu
from jax.sharding import PartitionSpec as P


def dot(left, right, left_dim, right_dim):
    return lax.dot_general(
        left,
        right,
        (((left_dim,), (right_dim,)), ((), ())),
        preferred_element_type=jnp.float32,
    )


def sigmoid(x):
    return 0.5 + 0.5 * jnp.tanh(0.5 * x)


def renorm(raw, target):
    scale = target * lax.rsqrt(jnp.sum(raw * raw, axis=0, keepdims=True) + 1e-06)
    return (raw * scale).astype(jnp.bfloat16)


def column_norm(weights):
    wide = weights.astype(jnp.float32)
    return jnp.sqrt(jnp.sum(wide * wide, axis=0, keepdims=True))


def chain_kernel(
    plan_ref, rows_ref, init_in_ref, init_out_ref, gain_ref, out_ref, w_in, w_out, norm_in, norm_out
):
    seg = pl.program_id(0)
    hidden_width = w_out.shape[0]

    @pl.when(seg == 0)
    def _():
        norm_in[...] = column_norm(init_in_ref[0])
        norm_out[...] = column_norm(init_out_ref[0])

    @pl.when(jnp.logical_or(seg == 0, plan_ref[2 + seg] == 1))
    def _():
        w_in[...] = init_in_ref[0]
        w_out[...] = init_out_ref[0]

    queries, keys, scaled = rows_ref[0, 0], rows_ref[0, 1], rows_ref[0, 2]
    pre = dot(keys, w_in[...], 1, 0)
    first, second = pre[:, :hidden_width], pre[:, hidden_width:]
    gate = sigmoid(first)
    act = first * gate
    hidden = (act * second).astype(jnp.bfloat16)
    grad_hidden = dot(scaled, w_out[...], 1, 1)
    grad_first = (grad_hidden * second * (gate + act * (1.0 - gate))).astype(jnp.bfloat16)
    grad_second = (grad_hidden * act).astype(jnp.bfloat16)
    grad_pre = jnp.concatenate([grad_first, grad_second], axis=1)
    new_in = renorm(w_in[...].astype(jnp.float32) + dot(keys, grad_pre, 0, 0), norm_in[...])
    new_out = renorm(w_out[...].astype(jnp.float32) + dot(hidden, scaled, 0, 0), norm_out[...])
    w_in[...] = new_in
    w_out[...] = new_out
    pre_q = dot(queries, new_in, 1, 0)
    first_q = pre_q[:, :hidden_width]
    hidden_q = (first_q * sigmoid(first_q) * pre_q[:, hidden_width:]).astype(jnp.bfloat16)
    fast = dot(hidden_q, new_out, 1, 0)
    spread = lax.rsqrt(jnp.mean(fast * fast, axis=1, keepdims=True) + 1e-05)
    out_ref[0] = (fast * spread * gain_ref[0]).astype(jnp.bfloat16)


def run_chain(plan, moved, init_in, init_out, gain):
    segs, _, rows, width = moved.shape
    wide, hidden_width = init_in.shape[2], init_out.shape[1]
    heads = gain.shape[0]
    turn = lambda s, plan: lax.rem(plan[0] + s, segs)
    flops = segs * rows * width * (wide * 3 + hidden_width * 3) * 2
    return pl.pallas_call(
        chain_kernel,
        out_shape=jax.ShapeDtypeStruct((segs, rows, width), jnp.bfloat16),
        grid_spec=pltpu.PrefetchScalarGridSpec(
            num_scalar_prefetch=1,
            grid=(segs,),
            in_specs=[
                pl.BlockSpec((1, 3, rows, width), lambda s, plan: (turn(s, plan), 0, 0, 0)),
                pl.BlockSpec((1, width, wide), lambda s, plan: (plan[1], 0, 0)),
                pl.BlockSpec((1, hidden_width, width), lambda s, plan: (plan[1], 0, 0)),
                pl.BlockSpec((1, 1, width), lambda s, plan: (plan[1], 0, 0)),
            ],
            out_specs=pl.BlockSpec((1, rows, width), lambda s, plan: (turn(s, plan), 0, 0)),
            scratch_shapes=[
                pltpu.VMEM((width, wide), jnp.bfloat16),
                pltpu.VMEM((hidden_width, width), jnp.bfloat16),
                pltpu.VMEM((1, wide), jnp.float32),
                pltpu.VMEM((1, width), jnp.float32),
            ],
        ),
        cost_estimate=pl.CostEstimate(
            flops=flops, bytes_accessed=2 * (moved.size + segs * rows * width), transcendentals=0
        ),
        name="chain",
    )(plan, moved, init_in, init_out, gain.reshape(heads, 1, width))


def shards(queries, keys, values, step_sizes, starts, resets, init_in, init_out, gain, out_proj):
    frames = lax.axis_size("frame")
    place = lax.axis_index("frame")
    videos, rows, _ = queries.shape
    heads, width, _ = init_in.shape
    per_set = max(1, min(videos, frames // heads))
    gain_heads = gain.reshape(heads, width)
    scaled = (
        values.reshape(videos, rows, heads, width).astype(jnp.float32)
        * step_sizes.astype(jnp.float32)[..., None]
    ).astype(jnp.bfloat16)
    head_here = lax.rem(place, heads)
    spread = []
    for first in range(0, videos, per_set):
        pick = lambda x: (
            x[first : first + per_set]
            .reshape(per_set, rows, heads, width)
            .transpose(0, 2, 1, 3)
            .reshape(per_set * heads, rows, width)
        )
        packed = jnp.stack([pick(queries), pick(keys), pick(scaled)], axis=1)
        packed = jnp.pad(packed, ((0, frames - per_set * heads), (0, 0), (0, 0), (0, 0)))
        spread.append(lax.all_to_all(packed, "frame", split_axis=0, concat_axis=0, tiled=True))
    normed = []
    for index, moved in enumerate(spread):
        video = index * per_set + jnp.minimum(place // heads, per_set - 1)
        plan = jnp.concatenate([starts[video][None], head_here[None], resets[video]])
        own = run_chain(plan.astype(jnp.int32), moved, init_in, init_out, gain_heads)
        back = lax.all_to_all(own, "frame", split_axis=0, concat_axis=0, tiled=True)
        normed.append(
            back[: per_set * heads]
            .reshape(per_set, heads, rows, width)
            .transpose(0, 2, 1, 3)
            .reshape(per_set * rows, heads * width)
        )
    parts = []
    for flat in normed:
        partial = jnp.dot(flat, out_proj, preferred_element_type=jnp.float32)
        parts.append(
            lax.psum_scatter(
                partial.astype(jnp.bfloat16), "head", scatter_dimension=1, tiled=True
            )
        )
    mixed = jnp.concatenate(parts, axis=0)
    return mixed.reshape(videos, rows, mixed.shape[1])


def solution(mesh):
    blocks = P(None, "frame", "head")
    return jax.shard_map(
        shards,
        mesh=mesh,
        in_specs=(
            blocks,
            blocks,
            blocks,
            blocks,
            P(),
            P(),
            P("head", None, None),
            P("head", None, None),
            P("head"),
            P("head", None),
        ),
        out_specs=blocks,
        check_vma=False,
    )
```
